128 devices in a mesh: dp: 32 (over z, y, x_hi), mod: 4 (over x_lo, core).
Axes of the slice: x: 4 (x_hi: 2, x_lo: 2; x = x_hi * 2 + x_lo), y: 4, z: 4, core: 2. Of those that a mesh axis runs over, the one named last changes fastest.
Arguments:
- embeddings: bfloat16 [4, 8192, 512], P('mod', 'dp'), may hold values from -4 to 4
- pairings: int32 [3, 4], replicated, may hold values from 0 to 3, as said below
- logit_scale: float32 [3], replicated, may hold values from 2 to 6
Outputs:
- gradient: float32 [4, 8192, 512], P('mod', 'dp')
- losses: float32 [4, 8192], P('mod', 'dp')
The draws below stay inside these ranges and needn't reach their ends.
Inputs may be any that keep to these rules, and one draw needn't show every extreme that they name: Row k of pairings maps each modality to its partner in matching k; each row is an involution without fixed points, and the three rows are the three perfect matchings of the four modalities in some order.
All inputs are finite; a program needn't handle non-finite values.
Results may differ from the reference program's by a relative error of at most 0.0013.
Values may be sent and summed in bfloat16 or wider, within the bound.
A program may use at most 192 MiB of HBM per device.

```python
import math
import jax
import jax.numpy as jnp
from jax import lax

D = 512
CLIP_DEV = 256
CLIPS = 8192
N_DP = 32


def draw_pairings(key, part):
    order = jax.random.permutation(jax.random.fold_in(key, 3), 3).astype(jnp.int32)
    modal = jnp.arange(4, dtype=jnp.int32)
    return jnp.bitwise_xor(modal[None, :], order[:, None] + 1).astype(jnp.int32)


def draw_embeddings(key, part):
    normed = D ** (-0.25)
    base = jnp.clip(jax.random.normal(jax.random.fold_in(key, 21), (4, CLIPS, D), jnp.float32), -5.0, 5.0) * normed
    return jnp.clip(base, -4.0, 4.0).astype(jnp.bfloat16)


def setup_inputs(seed: int = 0) -> dict:
    arg_keys = jax.random.split(jax.random.key(seed), 4)
    return {
        "embeddings": draw_embeddings(jax.random.fold_in(arg_keys[3], 71), 0),
        "pairings": draw_pairings(jax.random.fold_in(arg_keys[3], 71), 0),
        "logit_scale": jnp.clip(jnp.exp(jax.random.uniform(arg_keys[2], (3,), jnp.float32, math.log(2.0), math.log(6.0))), 2.0, 6.0),
    }


def score_block(anchor_rows, partner, factor):
    return factor * lax.dot_general(anchor_rows, partner, (((1,), (1,)), ((), ())), preferred_element_type=jnp.float32)


def pair_terms(anchor, partner, factor):
    anchor_blocks = anchor.reshape(N_DP, CLIP_DEV, D)
    partner_blocks = partner.reshape(N_DP, CLIP_DEV, D)

    def block_max(rows_in):
        return jnp.max(score_block(rows_in, partner, factor), 0)

    col_max = jnp.max(lax.map(block_max, anchor_blocks), 0)

    def block_sum(rows_in):
        return jnp.sum(jnp.exp(score_block(rows_in, partner, factor) - col_max[None, :]), 0)

    col_lse = col_max + jnp.log(jnp.sum(lax.map(block_sum, anchor_blocks), 0))

    def block_terms(pair_in):
        rows_in, own_rows = pair_in
        scores = score_block(rows_in, partner, factor)
        row_max = jnp.max(scores, 1, keepdims=True)
        row_lse = row_max[:, 0] + jnp.log(jnp.sum(jnp.exp(scores - row_max), 1))
        weights = (jnp.exp(scores - row_lse[:, None]) + jnp.exp(scores - col_lse[None, :])).astype(jnp.bfloat16)
        product = jnp.dot(weights, partner, preferred_element_type=jnp.float32)
        own_float = own_rows.astype(jnp.float32)
        diagonal = factor * jnp.sum(rows_in.astype(jnp.float32) * own_float, -1)
        return factor * (product - 2.0 * own_float), row_lse - diagonal

    grad_blocks, loss_blocks = lax.map(block_terms, (anchor_blocks, partner_blocks))
    return grad_blocks.reshape(CLIPS, D), loss_blocks.reshape(CLIPS)


def reference(embeddings, pairings, logit_scale):
    grad_list = []
    loss_list = []
    for modality in range(4):
        grad_total = jnp.zeros((CLIPS, D), jnp.float32)
        loss_total = jnp.zeros((CLIPS,), jnp.float32)
        for matching in range(3):
            partner_id = pairings[matching, modality].astype(jnp.int32)
            partner = lax.dynamic_index_in_dim(embeddings, partner_id, 0, keepdims=False)
            grad_part, loss_part = pair_terms(embeddings[modality], partner, logit_scale[matching])
            grad_total = grad_total + grad_part
            loss_total = loss_total + loss_part
        grad_list.append(grad_total)
        loss_list.append(loss_total)
    return (jnp.stack(grad_list), jnp.stack(loss_list))
```

```python
import jax
import jax.numpy as jnp
from jax import lax
from jax.sharding import PartitionSpec as P


def shards(embeddings, pairings, logit_scale):
    row_count = embeddings.shape[1]
    feat_width = embeddings.shape[2]
    mod_index = lax.axis_index("mod")
    anchor = embeddings[0]
    local_set = lax.all_gather(embeddings, "mod", axis=0, tiled=True)
    everything = lax.all_gather(local_set, "dp", axis=1, tiled=True)
    scores = []
    row_lse = []
    partners = []
    for matching in range(3):
        partner_id = pairings[matching][mod_index]
        partner = lax.dynamic_index_in_dim(everything, partner_id, 0, keepdims=False)
        score = logit_scale[matching] * lax.dot_general(
            anchor, partner, (((1,), (1,)), ((), ())), preferred_element_type=jnp.float32
        )
        row_max = jnp.max(score, 1, keepdims=True)
        row_lse.append(row_max[:, 0] + jnp.log(jnp.sum(jnp.exp(score - row_max), 1)))
        scores.append(score)
        partners.append(partner)
    stats = lax.all_gather(lax.all_gather(jnp.stack(row_lse)[None], "mod", axis=0, tiled=True), "dp", axis=2, tiled=True)
    gradient = jnp.zeros((row_count, feat_width), jnp.float32)
    losses = jnp.zeros((row_count,), jnp.float32)
    for matching in range(3):
        partner_id = pairings[matching][mod_index]
        factor = logit_scale[matching]
        own_rows = lax.dynamic_index_in_dim(local_set, partner_id, 0, keepdims=False)
        col_lse = lax.dynamic_index_in_dim(stats, partner_id, 0, keepdims=False)[matching]
        score = scores[matching]
        weights = (jnp.exp(score - row_lse[matching][:, None]) + jnp.exp(score - col_lse[None, :])).astype(jnp.bfloat16)
        product = jnp.dot(weights, partners[matching], preferred_element_type=jnp.float32)
        own_float = own_rows.astype(jnp.float32)
        diagonal = factor * jnp.sum(anchor.astype(jnp.float32) * own_float, -1)
        gradient = gradient + factor * (product - 2.0 * own_float)
        losses = losses + (row_lse[matching] - diagonal)
    return (gradient[None], losses[None])


def solution(mesh):
    return jax.shard_map(
        shards,
        mesh=mesh,
        in_specs=(P("mod", "dp", None), P(), P()),
        out_specs=(P("mod", "dp", None), P("mod", "dp")),
        check_vma=False,
    )
```

```python
import functools
import math

import jax
import jax.numpy as jnp
from jax import lax
from jax.experimental import pallas as pl
from jax.experimental.pallas import tpu as pltpu
from jax.sharding import PartitionSpec as P

MESH = pl.DeviceIdType.MESH
F32 = jnp.float32
BF16 = jnp.bfloat16
LN2 = math.log(2.0)
LOG2E = 1.0 / LN2
PART = F32


def kernel(
    pair_ref, scale_ref, emb_ref, grad_ref, loss_ref,
    cols, rows, scores, run_max, run_sum, acc, stage, relay, final,
    part, own_lse, col_lse, row_lse,
    local_sem, ag_send, ag_recv, sib_send, sib_recv, row_send, row_recv,
    part_send, part_recv, lse_send, lse_recv, rs_send, rs_recv,
):
    count, width = emb_ref.shape
    half, quarter = count // 2, count // 4
    dp = lax.axis_index("dp")
    mod = lax.axis_index("mod")
    x_hi, y, z = dp % 2, (dp // 2) % 4, dp // 8
    core, x_lo = mod % 2, mod // 2
    x = x_hi * 2 + x_lo

    def device(dx=0, dy=0, dz=0, dc=0):
        xx, yy, zz, cc = (x + dx) % 4, (y + dy) % 4, (z + dz) % 4, (core + dc) % 2
        return {"dp": (zz * 4 + yy) * 2 + xx // 2, "mod": (xx % 2) * 2 + cc}

    def partner(q):
        return ((x_lo + q // 2) % 2) * 2 + (core + q % 2) % 2

    def factor(q):
        p = partner(q)
        total = jnp.float32(0.0)
        for k in range(3):
            total = total + jnp.where(pair_ref[k, mod] == p, scale_ref[k], jnp.float32(0.0))
        return total

    def remote(src, dst, send, recv, to):
        return pltpu.make_async_remote_copy(
            src_ref=src, dst_ref=dst, send_sem=send, recv_sem=recv, device_id=to, device_id_type=MESH
        )

    barrier = pltpu.get_barrier_semaphore()
    peers = [device(dz=1), device(dz=3), device(dy=1), device(dy=2), device(dy=3)]
    for q in (1, 2, 3):
        for block in range(8):
            peers.append({"dp": ((block % 4) * 4 + y) * 2 + block // 4, "mod": partner(q)})
    for peer in peers:
        pl.semaphore_signal(barrier, inc=1, device_id=peer, device_id_type=MESH)

    def block_of(dx, dz):
        xx, zz = (x + dx) % 4, (z + dz) % 4
        return xx % 2, (xx // 2) * 4 + zz

    def piece(dx, dz, start, size, dc=0):
        lo, block = block_of(dx, dz)
        return cols.at[lo * 2 + (core + dc) % 2, pl.ds(pl.multiple_of(block * count + start, 64), size), :]

    fill_cols = pltpu.make_async_copy(emb_ref, piece(0, 0, 0, count), local_sem.at[0])
    fill_rows = pltpu.make_async_copy(emb_ref, rows.at[y], local_sem.at[1])
    fill_cols.start()
    fill_rows.start()
    run_max[...] = jnp.full(run_max.shape, -1e30, F32)
    run_sum[...] = jnp.zeros(run_sum.shape, F32)
    pl.semaphore_wait(barrier, len(peers))

    EVENTS = ((-1, 0, half, 1), (1, 0, half, -1), (2, 0, quarter, 1), (2, quarter, quarter, -1))

    def offsets(h, a, b):
        return (a, b) if h == 0 else (b, a)

    def place(h, group, event):
        rel, start, size, way = EVENTS[event]
        a, b = (rel, 0) if group == 0 else ((0, -1, 1, 2)[group - 1], rel)
        dx, dz = offsets(h, a, b)
        along_x = (group == 0) == (h == 0)
        return dx, dz, h * half + start, size, way, along_x

    def ag_copy(h, group, event):
        dx, dz, start, size, way, along_x = place(h, group, event)
        to = device(dx=way) if along_x else device(dz=way)
        sx, sz = (dx + way, dz) if along_x else (dx, dz + way)
        src = piece(sx, sz, start, size)
        if group in (0, 1) and event in (0, 1):
            src = emb_ref.at[pl.ds(start, size), :]
        return remote(src, piece(sx, sz, start, size), ag_send.at[h, group, event], ag_recv.at[h, group, event], to)

    def ag_arrival(h, group, event):
        dx, dz, start, size, _, _ = place(h, group, event)
        region = piece(dx, dz, start, size)
        return remote(region, region, ag_send.at[h, group, event], ag_recv.at[h, group, event], device(dc=1))

    def sib_copy(h, group, event, dc=0):
        dx, dz, start, size, _, _ = place(h, group, event)
        region = piece(dx, dz, start, size, dc)
        return remote(region, region, sib_send.at[h, group, event], sib_recv.at[h, group, event], device(dc=1))

    def sib_own(dc=0):
        region = piece(0, 0, 0, count, dc)
        src = region if dc else emb_ref
        return remote(src, region, sib_send.at[0, 5, 0], sib_recv.at[0, 5, 0], device(dc=1))

    row_spans = ((1, 0, count, 1), (-1, 0, count, -1), (2, 0, half, 1), (2, half, half, -1))

    def row_copy(event, arrival=False):
        rel, start, size, way = row_spans[event]
        owner = y - way if event >= 2 else y
        if arrival:
            owner = y + (2 if event >= 2 else -way)
        region = rows.at[(owner + 4) % 4, pl.ds(start, size), :]
        src = emb_ref if event < 2 and not arrival else region
        return remote(src, region, row_send.at[event], row_recv.at[event], device(dy=way))

    started = []

    def go(copy):
        copy.start()
        started.append(copy)

    def forward_to_sibling(group, events):
        for h in (0, 1):
            for event in events:
                go(sib_copy(h, group, event))

    def arrive(group, events):
        for h in (0, 1):
            for event in events:
                ag_arrival(h, group, event).wait_recv()

    def send(group, events):
        for h in (0, 1):
            for event in events:
                go(ag_copy(h, group, event))

    def sib_arrive(group, events):
        for h in (0, 1):
            for event in events:
                sib_copy(h, group, event, 1).wait_recv()

    def units(n, decode):
        def body(step, carry):
            i, r = step // 4, step % 4
            q, dx, dz = decode(i)
            lo, block = block_of(dx, dz)
            p = partner(q)
            scale = factor(q) * jnp.float32(LOG2E)
            here = pl.ds(pl.multiple_of(block * count, count), count)
            these = pl.ds(pl.multiple_of(r * count, count), count)
            t = scale * lax.dot_general(
                rows[r], cols[p, here, :], (((1,), (1,)), ((), ())), preferred_element_type=F32
            )
            scores[q - 1, these, here] = t
            old = run_max[q - 1, these, :]
            new = old
            for lane in range(0, count, 128):
                new = jnp.maximum(new, t[:, lane:lane + 128])
            total = run_sum[q - 1, these, :] * jnp.exp2(old - new)
            for lane in range(0, count, 128):
                total = total + jnp.exp2(t[:, lane:lane + 128] - new)
            run_max[q - 1, these, :] = new
            run_sum[q - 1, these, :] = total
            return carry

        lax.fori_loop(0, n * 4, body, 0)

    near, far = (0, 1), (2, 3)
    send(0, near)
    go(sib_own())
    go(row_copy(0))
    go(row_copy(1))
    send(1, near)
    fill_cols.wait()
    fill_rows.wait()
    arrive(0, near)
    send(0, far)
    send(2, near)
    send(3, near)
    forward_to_sibling(0, near)
    row_copy(0, True).wait_recv()
    row_copy(1, True).wait_recv()
    go(row_copy(2))
    go(row_copy(3))
    arrive(1, near)
    send(1, far)
    forward_to_sibling(1, near)
    arrive(0, far)
    send(4, near)
    forward_to_sibling(0, far)
    row_copy(2, True).wait_recv()
    row_copy(3, True).wait_recv()
    arrive(2, near)
    send(2, far)
    forward_to_sibling(2, near)
    sib_own(1).wait_recv()
    sib_arrive(0, near)
    sib_arrive(1, near)
    units(3, lambda i: (1, 0, i + 3))
    arrive(3, near)
    send(3, far)
    forward_to_sibling(3, near)
    units(4, lambda i: (2 + i // 2, 1 + 2 * (i % 2), 0))
    arrive(1, far)
    forward_to_sibling(1, far)
    sib_arrive(2, near)
    sib_arrive(3, near)
    units(4, lambda i: (2 + i // 4, 1 + 2 * (i % 2), 1 + 2 * ((i // 2) % 2)))
    arrive(4, near)
    send(4, far)
    forward_to_sibling(4, near)
    units(4, lambda i: (3, 1 + 2 * (i % 2), 1 + 2 * ((i // 2) % 2)))
    arrive(2, far)
    forward_to_sibling(2, far)
    arrive(3, far)
    forward_to_sibling(3, far)
    sib_arrive(0, far)
    sib_arrive(1, far)
    units(2, lambda i: (1, 2 * i, 2 * (1 - i)))
    arrive(4, far)
    forward_to_sibling(4, far)
    sib_arrive(2, far)
    sib_arrive(3, far)
    sib_arrive(4, near)
    units(4, lambda i: (2 + i // 2, 1 + 2 * (i % 2), 2))
    sib_arrive(4, far)
    units(3, lambda i: (1, 2, i + 1))

    def reduce_stats(step, carry):
        q, r, g = step // 8, (step // 2) % 4, step % 2
        these = pl.ds(pl.multiple_of(r * count + g * 128, 128), 128)
        m_t = run_max[q, these, :].T
        s_t = run_sum[q, these, :].T
        top = jnp.max(m_t, axis=0, keepdims=True)
        total = jnp.sum(s_t * jnp.exp2(m_t - top), axis=0, keepdims=True)
        lanes = pl.ds(pl.multiple_of(g * 128, 128), 128)
        part[y, r, q, :, lanes] = top
        part[y, r, q + 3, :, lanes] = total
        return carry

    lax.fori_loop(0, 24, reduce_stats, 0)

    def part_copy(shift, owner):
        region = part.at[owner]
        return remote(region, region, part_send.at[shift - 1], part_recv.at[shift - 1], device(dy=shift))

    for shift in (2, 1, 3):
        go(part_copy(shift, y))
    for shift in (1, 3, 2):
        part_copy(shift, (y + 4 - shift) % 4).wait_recv()
    for q in range(3):
        top = part[0, :, q]
        for member in range(1, 4):
            top = jnp.maximum(top, part[member, :, q])
        total = jnp.zeros_like(top)
        for member in range(4):
            total = total + part[member, :, q + 3] * jnp.exp2(part[member, :, q] - top)
        row_lse[q] = top + jnp.log2(total)
        own_lse[q] = row_lse[q, y]

    my_block = x_hi * 4 + z

    def lse_copy(q, block, source):
        to = {"dp": ((block % 4) * 4 + y) * 2 + block // 4, "mod": partner(q)}
        return remote(
            own_lse.at[q - 1], col_lse.at[q - 1, source], lse_send.at[q - 1, block], lse_recv.at[q - 1, source], to
        )

    for q in (1, 2, 3):
        for block in range(8):
            go(lse_copy(q, block, my_block))

    def spread(step, carry):
        q, r, g = step // 8, (step // 2) % 4, step % 2
        lanes = pl.ds(pl.multiple_of(g * 128, 128), 128)
        these = pl.ds(pl.multiple_of(r * count + g * 128, 128), 128)
        value = jnp.broadcast_to(row_lse[q, r, :, lanes], (128, 128))
        run_max[q, these, :] = value.T
        return carry

    lax.fori_loop(0, 24, spread, 0)
    loss = jnp.zeros((1, count), F32)
    eye = lax.broadcasted_iota(jnp.int32, (count, count), 0) == lax.broadcasted_iota(jnp.int32, (count, count), 1)
    own_rows = pl.ds(pl.multiple_of(y * count, count), count)
    own_cols = pl.ds(pl.multiple_of(my_block * count, count), count)
    for q in range(3):
        tile = scores[q, own_rows, own_cols]
        diagonal = jnp.sum(jnp.where(eye, tile, 0.0), axis=0, keepdims=True)
        loss = loss + (own_lse[q] - diagonal) * LN2
    loss_ref[...] = loss

    for q in (1, 2, 3):
        for block in range(8):
            lse_copy(q, block, block).wait_recv()

    span = 4

    def product(r):
        these = pl.ds(pl.multiple_of(r * count, count), count)

        def body(step, carry):
            q, c = step // (8 // span) + 1, step % (8 // span)
            p = partner(q)
            pieces = []
            row_value = run_max[q - 1, these, :]
            for b in range(span):
                column = col_lse[q - 1, c * span + b]
                for lane in range(0, count, 128):
                    t = scores[q - 1, these, pl.ds(pl.multiple_of((c * span + b) * count + lane, 128), 128)]
                    w = jnp.exp2(t - row_value) + jnp.exp2(t - column[:, lane:lane + 128])
                    pieces.append(w.astype(BF16))
            weights = jnp.concatenate(pieces, axis=1)
            here = pl.ds(pl.multiple_of(c * (span * count), span * count), span * count)
            out = factor(q) * jnp.dot(weights, cols[p, here, :], preferred_element_type=F32)
            acc[r] = acc[r] + out
            return carry

        acc[r] = jnp.zeros((count, width), F32)
        lax.fori_loop(0, 3 * (8 // span), body, 0)

    up, down, across = (y + 1) % 4, (y + 3) % 4, (y + 2) % 4

    def rs_copy(kind, src, dst, way):
        slot = 0 if way == 1 else 1
        return remote(src, dst, rs_send.at[slot, kind], rs_recv.at[slot, kind], device(dy=way))

    lower, upper = pl.ds(0, half), pl.ds(half, half)
    product(across)
    stage[0] = acc[across].astype(PART)
    go(rs_copy(0, stage.at[0, lower, :], relay.at[0], 1))
    go(rs_copy(0, stage.at[0, upper, :], relay.at[1], -1))
    product(up)
    stage[1, half:, :] = acc[up, half:, :].astype(PART)
    go(rs_copy(1, stage.at[1, upper, :], final.at[0, upper, :], 1))
    product(down)
    stage[2, :half, :] = acc[down, :half, :].astype(PART)
    go(rs_copy(1, stage.at[2, lower, :], final.at[1, lower, :], -1))
    rs_copy(0, relay.at[0], relay.at[0], 1).wait_recv()
    stage[1, :half, :] = (acc[up, :half, :] + relay[0].astype(F32)).astype(PART)
    go(rs_copy(2, stage.at[1, lower, :], final.at[0, lower, :], 1))
    rs_copy(0, relay.at[1], relay.at[1], -1).wait_recv()
    stage[2, half:, :] = (acc[down, half:, :] + relay[1].astype(F32)).astype(PART)
    go(rs_copy(2, stage.at[2, upper, :], final.at[1, upper, :], -1))
    product(y)
    own = jnp.zeros((count, width), F32)
    for q in (1, 2, 3):
        own = own + (2.0 * factor(q)) * cols[partner(q), own_cols, :].astype(F32)
    acc[y] = acc[y] - own
    rs_copy(1, final.at[0, upper, :], final.at[0, upper, :], 1).wait_recv()
    rs_copy(1, final.at[1, lower, :], final.at[1, lower, :], -1).wait_recv()
    rs_copy(2, final.at[0, lower, :], final.at[0, lower, :], 1).wait_recv()
    rs_copy(2, final.at[1, upper, :], final.at[1, upper, :], -1).wait_recv()
    grad_ref[...] = acc[y] + (final[0].astype(F32) + final[1].astype(F32))
    for copy in started:
        copy.wait_send()


def solution(mesh):
    def shards(embeddings, pairings, logit_scale):
        _, count, width = embeddings.shape
        dma = pltpu.SemaphoreType.DMA
        grad, loss = pl.pallas_call(
            kernel,
            out_shape=(
                jax.ShapeDtypeStruct((count, width), F32),
                jax.ShapeDtypeStruct((1, count), F32),
            ),
            in_specs=[
                pl.BlockSpec(memory_space=pltpu.SMEM),
                pl.BlockSpec(memory_space=pltpu.SMEM),
                pl.BlockSpec(memory_space=pltpu.VMEM),
            ],
            out_specs=(pl.BlockSpec(memory_space=pltpu.VMEM), pl.BlockSpec(memory_space=pltpu.VMEM)),
            scratch_shapes=[
                pltpu.VMEM((4, 8 * count, width), BF16),
                pltpu.VMEM((4, count, width), BF16),
                pltpu.VMEM((3, 4 * count, 8 * count), F32),
                pltpu.VMEM((3, 4 * count, 128), F32),
                pltpu.VMEM((3, 4 * count, 128), F32),
                pltpu.VMEM((4, count, width), F32),
                pltpu.VMEM((3, count, width), PART),
                pltpu.VMEM((2, count // 2, width), PART),
                pltpu.VMEM((2, count, width), PART),
                pltpu.VMEM((4, 4, 6, 1, count), F32),
                pltpu.VMEM((3, 1, count), F32),
                pltpu.VMEM((3, 8, 1, count), F32),
                pltpu.VMEM((3, 4, 1, count), F32),
                dma((2,)),
                dma((2, 5, 4)),
                dma((2, 5, 4)),
                dma((2, 6, 4)),
                dma((2, 6, 4)),
                dma((4,)),
                dma((4,)),
                dma((3,)),
                dma((3,)),
                dma((3, 8)),
                dma((3, 8)),
                dma((2, 3)),
                dma((2, 3)),
            ],
            compiler_params=pltpu.CompilerParams(
                collective_id=0, has_side_effects=True, vmem_limit_bytes=60 * 1024 * 1024
            ),
        )(pairings, logit_scale, embeddings[0])
        return grad[None], loss

    return jax.shard_map(
        shards,
        mesh=mesh,
        in_specs=(P("mod", "dp", None), P(), P()),
        out_specs=(P("mod", "dp", None), P("mod", "dp")),
        check_vma=False,
    )
```

```python
import functools
import math

import jax
import jax.numpy as jnp
from jax import lax
from jax.experimental import pallas as pl
from jax.experimental.pallas import tpu as pltpu
from jax.sharding import PartitionSpec as P

MESH = pl.DeviceIdType.MESH
F32 = jnp.float32
BF16 = jnp.bfloat16
LN2 = math.log(2.0)
LOG2E = 1.0 / LN2
PART = BF16


def kernel(
    pair_ref, scale_ref, emb_ref, grad_ref, loss_ref,
    cols, rows, scores, run_max, run_sum, acc, stage, relay, final,
    part_a, part_b, own_lse, col_lse, row_lse,
    local_sem, ag_send, ag_recv, sib_send, sib_recv, row_send, row_recv,
    part_send, part_recv, lse_send, lse_recv, rs_send, rs_recv,
):
    count, width = emb_ref.shape
    half, quarter = count // 2, count // 4
    dp = lax.axis_index("dp")
    mod = lax.axis_index("mod")
    x_hi, y, z = dp % 2, (dp // 2) % 4, dp // 8
    core, x_lo = mod % 2, mod // 2
    x = x_hi * 2 + x_lo

    def device(dx=0, dy=0, dz=0, dc=0):
        xx, yy, zz, cc = (x + dx) % 4, (y + dy) % 4, (z + dz) % 4, (core + dc) % 2
        return {"dp": (zz * 4 + yy) * 2 + xx // 2, "mod": (xx % 2) * 2 + cc}

    def partner(q):
        return ((x_lo + q // 2) % 2) * 2 + (core + q % 2) % 2

    def factor(q):
        p = partner(q)
        total = jnp.float32(0.0)
        for k in range(3):
            total = total + jnp.where(pair_ref[k, mod] == p, scale_ref[k], jnp.float32(0.0))
        return total

    def remote(src, dst, send, recv, to):
        return pltpu.make_async_remote_copy(
            src_ref=src, dst_ref=dst, send_sem=send, recv_sem=recv, device_id=to, device_id_type=MESH
        )

    barrier = pltpu.get_barrier_semaphore()
    peers = [device(dx=1), device(dx=3), device(dy=1), device(dy=3), device(dz=1), device(dz=3), device(dc=1)]
    for peer in peers:
        pl.semaphore_signal(barrier, inc=1, device_id=peer, device_id_type=MESH)

    def block_of(dx, dz):
        xx, zz = (x + dx) % 4, (z + dz) % 4
        return xx % 2, (xx // 2) * 4 + zz

    def piece(dx, dz, start, size, dc=0):
        lo, block = block_of(dx, dz)
        return cols.at[lo * 2 + (core + dc) % 2, pl.ds(pl.multiple_of(block * count + start, 64), size), :]

    fill_cols = pltpu.make_async_copy(emb_ref, piece(0, 0, 0, count), local_sem.at[0])
    fill_rows = pltpu.make_async_copy(emb_ref, rows.at[y], local_sem.at[1])
    fill_cols.start()
    fill_rows.start()
    run_max[...] = jnp.full(run_max.shape, -1e30, F32)
    run_sum[...] = jnp.zeros(run_sum.shape, F32)
    acc[...] = jnp.zeros(acc.shape, F32)
    pl.semaphore_wait(barrier, len(peers))

    EVENTS = ((-1, 0, half, 1), (1, 0, half, -1), (2, 0, quarter, 1), (2, quarter, quarter, -1))

    def offsets(h, a, b):
        return (a, b) if h == 0 else (b, a)

    def place(h, group, event):
        rel, start, size, way = EVENTS[event]
        a, b = (rel, 0) if group == 0 else ((0, -1, 1, 2)[group - 1], rel)
        dx, dz = offsets(h, a, b)
        along_x = (group == 0) == (h == 0)
        return dx, dz, h * half + start, size, way, along_x

    def ag_copy(h, group, event):
        dx, dz, start, size, way, along_x = place(h, group, event)
        to = device(dx=way) if along_x else device(dz=way)
        sx, sz = (dx + way, dz) if along_x else (dx, dz + way)
        src = piece(sx, sz, start, size)
        if group in (0, 1) and event in (0, 1):
            src = emb_ref.at[pl.ds(start, size), :]
        return remote(src, piece(sx, sz, start, size), ag_send.at[h, group, event], ag_recv.at[h, group, event], to)

    def ag_arrival(h, group, event):
        dx, dz, start, size, _, _ = place(h, group, event)
        region = piece(dx, dz, start, size)
        return remote(region, region, ag_send.at[h, group, event], ag_recv.at[h, group, event], device(dc=1))

    def sib_copy(h, group, event, dc=0):
        dx, dz, start, size, _, _ = place(h, group, event)
        region = piece(dx, dz, start, size, dc)
        return remote(region, region, sib_send.at[h, group, event], sib_recv.at[h, group, event], device(dc=1))

    def sib_own(dc=0):
        region = piece(0, 0, 0, count, dc)
        src = region if dc else emb_ref
        return remote(src, region, sib_send.at[0, 5, 0], sib_recv.at[0, 5, 0], device(dc=1))

    row_spans = ((1, 0, count, 1), (-1, 0, count, -1), (2, 0, half, 1), (2, half, half, -1))

    def row_copy(event, arrival=False):
        rel, start, size, way = row_spans[event]
        owner = y - way if event >= 2 else y
        if arrival:
            owner = y + (2 if event >= 2 else -way)
        region = rows.at[(owner + 4) % 4, pl.ds(start, size), :]
        src = emb_ref if event < 2 and not arrival else region
        return remote(src, region, row_send.at[event], row_recv.at[event], device(dy=way))

    started = []

    def go(copy):
        copy.start()
        started.append(copy)

    def to_sibling(*triples):
        for triple in triples:
            go(sib_copy(*triple))

    def arrive(*triples):
        for triple in triples:
            ag_arrival(*triple).wait_recv()

    def send(*triples):
        for triple in triples:
            go(ag_copy(*triple))

    def sib_arrive(*triples):
        for triple in triples:
            sib_copy(*triple, 1).wait_recv()

    def near(h, group):
        return (h, group, 0), (h, group, 1)

    def far(h, group):
        return (h, group, 2), (h, group, 3)

    def pairs(n, decode):
        def body(i, carry):
            q, dx0, dz0, dx1, dz1 = decode(i)
            p = partner(q)
            scale = factor(q) * jnp.float32(LOG2E)
            heres = []
            for dx, dz in ((dx0, dz0), (dx1, dz1)):
                heres.append(pl.ds(pl.multiple_of(block_of(dx, dz)[1] * count, count), count))
            for r in range(4):
                these = pl.ds(r * count, count)
                lanes = []
                for here in heres:
                    t = scale * lax.dot_general(
                        rows[r], cols[p, here, :], (((1,), (1,)), ((), ())), preferred_element_type=F32
                    )
                    scores[q - 1, these, here] = t
                    lanes += [t[:, lane:lane + 128] for lane in range(0, count, 128)]
                old = run_max[q - 1, these, :]
                new = old
                for t in lanes:
                    new = jnp.maximum(new, t)
                total = run_sum[q - 1, these, :] * jnp.exp2(old - new)
                for t in lanes:
                    total = total + jnp.exp2(t - new)
                run_max[q - 1, these, :] = new
                run_sum[q - 1, these, :] = total
            return carry

        lax.fori_loop(0, n, body, 0)

    def reduce_stats(first, n, part):
        def body(step, carry):
            q, r = step // 4, step % 4
            for g in range(count // 128):
                these = pl.ds(pl.multiple_of(r * count + g * 128, 128), 128)
                m_t = run_max[first - 1 + q, these, :].T
                s_t = run_sum[first - 1 + q, these, :].T
                top = jnp.max(m_t, axis=0, keepdims=True)
                total = jnp.sum(s_t * jnp.exp2(m_t - top), axis=0, keepdims=True)
                lanes = pl.ds(g * 128, 128)
                part[y, r, q, :, lanes] = top
                part[y, r, q + n, :, lanes] = total
            return carry

        lax.fori_loop(0, n * 4, body, 0)

    def part_copy(part, sem, shift, owner):
        region = part.at[owner]
        return remote(region, region, part_send.at[sem, shift - 1], part_recv.at[sem, shift - 1], device(dy=shift))

    def send_part(part, sem):
        for shift in (2, 1, 3):
            go(part_copy(part, sem, shift, y))

    my_block = x_hi * 4 + z

    def lse_copy(q, block, source):
        to = {"dp": ((block % 4) * 4 + y) * 2 + block // 4, "mod": partner(q)}
        return remote(
            own_lse.at[q - 1], col_lse.at[q - 1, source], lse_send.at[q - 1, block], lse_recv.at[q - 1, source], to
        )

    def combine(first, n, part, sem):
        for shift in (1, 3, 2):
            part_copy(part, sem, shift, (y + 4 - shift) % 4).wait_recv()
        for q in range(n):
            top = part[0, :, q]
            for member in range(1, 4):
                top = jnp.maximum(top, part[member, :, q])
            total = jnp.zeros_like(top)
            for member in range(4):
                total = total + part[member, :, q + n] * jnp.exp2(part[member, :, q] - top)
            row_lse[first - 1 + q] = top + jnp.log2(total)
            own_lse[first - 1 + q] = row_lse[first - 1 + q, y]
        for q in range(first, first + n):
            for block in range(8):
                go(lse_copy(q, block, my_block))

        def spread(step, carry):
            q, r = first - 1 + step // 4, step % 4
            for g in range(count // 128):
                lanes = pl.ds(g * 128, 128)
                these = pl.ds(pl.multiple_of(r * count + g * 128, 128), 128)
                value = jnp.broadcast_to(row_lse[q, r, :, lanes], (128, 128))
                run_max[q, these, :] = value.T
            return carry

        lax.fori_loop(0, 4 * n, spread, 0)

    def columns_arrive(first, n):
        for q in range(first, first + n):
            for block in range(8):
                lse_copy(q, block, block).wait_recv()

    def product(q, r):
        these = pl.ds(pl.multiple_of(r * count, count), count)
        row_value = run_max[q - 1, these, :]
        pieces = []
        for block in range(8):
            column = col_lse[q - 1, block]
            for lane in range(0, count, 128):
                t = scores[q - 1, these, block * count + lane:block * count + lane + 128]
                w = jnp.exp2(t - row_value) + jnp.exp2(t - column[:, lane:lane + 128])
                pieces.append(w.astype(BF16))
        out = jnp.dot(jnp.concatenate(pieces, axis=1), cols[partner(q)], preferred_element_type=F32)
        acc[r] = acc[r] + factor(q) * out

    send(*near(0, 0), *near(1, 0))
    go(sib_own())
    go(row_copy(0))
    go(row_copy(1))
    send(*near(1, 1), *near(0, 1))
    fill_cols.wait()
    fill_rows.wait()
    arrive(*near(0, 0), *near(1, 0))
    send(*far(1, 0), *near(1, 2), *near(0, 2), *far(0, 0), *near(0, 3), *near(1, 3))
    to_sibling(*near(0, 0), *near(1, 0))
    arrive(*near(0, 1), *near(1, 1))
    to_sibling(*near(1, 1), *near(0, 1))
    row_copy(0, True).wait_recv()
    row_copy(1, True).wait_recv()
    go(row_copy(2))
    go(row_copy(3))
    arrive(*far(1, 0))
    send(*near(1, 4))
    to_sibling(*far(1, 0))
    arrive(*near(1, 2))
    to_sibling(*near(1, 2))
    arrive(*near(0, 2))
    send(*far(0, 2))
    to_sibling(*near(0, 2))
    arrive(*far(0, 0))
    to_sibling(*far(0, 0))
    row_copy(2, True).wait_recv()
    row_copy(3, True).wait_recv()
    sib_arrive(*near(0, 0), *near(1, 1))
    pairs(2, lambda i: (2 + i, 1, 0, 3, 0))
    arrive(*near(0, 3))
    send(*far(0, 3), *near(0, 4), *far(0, 1))
    to_sibling(*near(0, 3))
    arrive(*near(1, 3))
    send(*far(1, 1), *far(1, 2), *far(1, 3))
    to_sibling(*near(1, 3))
    pairs(2, lambda i: (2, 1, 1 + 2 * i, 3, 1 + 2 * i))
    sib_arrive(*near(0, 2), *near(0, 3), *near(1, 2), *near(1, 3))
    pairs(1, lambda i: (3, 1, 1, 3, 1))
    arrive(*near(1, 4))
    send(*far(1, 4))
    to_sibling(*near(1, 4))
    arrive(*far(0, 2), *far(0, 3))
    to_sibling(*far(0, 2), *far(0, 3))
    pairs(2, lambda i: (3 - i, 1, 3 - i, 3, 3 - i))
    sib_arrive(*near(1, 4), *far(0, 2), *far(0, 3))
    pairs(1, lambda i: (3, 1, 2, 3, 2))
    arrive(*near(0, 4))
    send(*far(0, 4))
    to_sibling(*near(0, 4))
    reduce_stats(2, 2, part_a)
    send_part(part_a, 0)
    arrive(*far(1, 1), *far(0, 1), *far(1, 2))
    to_sibling(*far(1, 1), *far(0, 1), *far(1, 2))
    sib_own(1).wait_recv()
    sib_arrive(*near(1, 0), *near(0, 1))
    pairs(1, lambda i: (1, 0, 1, 0, 3))
    arrive(*far(1, 3))
    to_sibling(*far(1, 3))
    sib_arrive(*far(1, 0), *far(0, 0), *far(1, 1), *far(0, 1))
    pairs(1, lambda i: (1, 0, 2, 2, 0))
    arrive(*far(1, 4), *far(0, 4))
    to_sibling(*far(1, 4), *far(0, 4))
    sib_arrive(*near(0, 4), *far(1, 2), *far(1, 3))
    pairs(1, lambda i: (1, 2, 1, 2, 3))
    sib_arrive(*far(1, 4), *far(0, 4))
    pairs(1, lambda i: (1, 0, 0, 2, 2))
    reduce_stats(1, 1, part_b)
    send_part(part_b, 1)
    combine(2, 2, part_a, 0)
    combine(1, 1, part_b, 1)

    loss = jnp.zeros((1, count), F32)
    eye = lax.broadcasted_iota(jnp.int32, (count, count), 0) == lax.broadcasted_iota(jnp.int32, (count, count), 1)
    own_rows = pl.ds(pl.multiple_of(y * count, count), count)
    own_cols = pl.ds(pl.multiple_of(my_block * count, count), count)
    for q in range(3):
        tile = scores[q, own_rows, own_cols]
        diagonal = jnp.sum(jnp.where(eye, tile, 0.0), axis=0, keepdims=True)
        loss = loss + (own_lse[q] - diagonal) * LN2
    loss_ref[...] = loss
    own = jnp.zeros((count, width), F32)
    for q in (1, 2, 3):
        own = own + (2.0 * factor(q)) * cols[partner(q), own_cols, :].astype(F32)
    acc[y] = acc[y] - own

    up, down, across = (y + 1) % 4, (y + 3) % 4, (y + 2) % 4

    def rs_copy(kind, src, dst, way):
        slot = 0 if way == 1 else 1
        return remote(src, dst, rs_send.at[slot, kind], rs_recv.at[slot, kind], device(dy=way))

    lower, upper = pl.ds(0, half), pl.ds(half, half)

    def early(step, carry):
        i = step // 2
        product(2 + step % 2, (y + 2 - i + 3 * (i // 2)) % 4)
        return carry

    def late(q, r):
        def body(step, carry):
            product(q + step, r)
            return carry
        return body

    columns_arrive(2, 2)
    lax.fori_loop(0, 6, early, 0)
    columns_arrive(1, 1)
    lax.fori_loop(0, 1, late(1, across), 0)
    stage[0] = acc[across].astype(PART)
    go(rs_copy(0, stage.at[0, lower, :], relay.at[0], 1))
    go(rs_copy(0, stage.at[0, upper, :], relay.at[1], -1))
    lax.fori_loop(0, 1, late(1, up), 0)
    stage[1, half:, :] = acc[up, half:, :].astype(PART)
    go(rs_copy(1, stage.at[1, upper, :], final.at[0, upper, :], 1))
    lax.fori_loop(0, 1, late(1, down), 0)
    stage[2, :half, :] = acc[down, :half, :].astype(PART)
    go(rs_copy(1, stage.at[2, lower, :], final.at[1, lower, :], -1))
    lax.fori_loop(0, 1, late(1, y), 0)
    rs_copy(0, relay.at[0], relay.at[0], 1).wait_recv()
    stage[1, :half, :] = (acc[up, :half, :] + relay[0].astype(F32)).astype(PART)
    go(rs_copy(2, stage.at[1, lower, :], final.at[0, lower, :], 1))
    rs_copy(0, relay.at[1], relay.at[1], -1).wait_recv()
    stage[2, half:, :] = (acc[down, half:, :] + relay[1].astype(F32)).astype(PART)
    go(rs_copy(2, stage.at[2, upper, :], final.at[1, upper, :], -1))
    lax.fori_loop(0, 2, late(2, y), 0)
    rs_copy(1, final.at[0, upper, :], final.at[0, upper, :], 1).wait_recv()
    rs_copy(1, final.at[1, lower, :], final.at[1, lower, :], -1).wait_recv()
    rs_copy(2, final.at[0, lower, :], final.at[0, lower, :], 1).wait_recv()
    rs_copy(2, final.at[1, upper, :], final.at[1, upper, :], -1).wait_recv()
    grad_ref[...] = acc[y] + (final[0].astype(F32) + final[1].astype(F32))
    for copy in started:
        copy.wait_send()


def solution(mesh):
    def shards(embeddings, pairings, logit_scale):
        _, count, width = embeddings.shape
        dma = pltpu.SemaphoreType.DMA
        grad, loss = pl.pallas_call(
            kernel,
            out_shape=(
                jax.ShapeDtypeStruct((count, width), F32),
                jax.ShapeDtypeStruct((1, count), F32),
            ),
            in_specs=[
                pl.BlockSpec(memory_space=pltpu.SMEM),
                pl.BlockSpec(memory_space=pltpu.SMEM),
                pl.BlockSpec(memory_space=pltpu.VMEM),
            ],
            out_specs=(pl.BlockSpec(memory_space=pltpu.VMEM), pl.BlockSpec(memory_space=pltpu.VMEM)),
            scratch_shapes=[
                pltpu.VMEM((4, 8 * count, width), BF16),
                pltpu.VMEM((4, count, width), BF16),
                pltpu.VMEM((3, 4 * count, 8 * count), F32),
                pltpu.VMEM((3, 4 * count, 128), F32),
                pltpu.VMEM((3, 4 * count, 128), F32),
                pltpu.VMEM((4, count, width), F32),
                pltpu.VMEM((3, count, width), PART),
                pltpu.VMEM((2, count // 2, width), PART),
                pltpu.VMEM((2, count, width), PART),
                pltpu.VMEM((4, 4, 4, 1, count), F32),
                pltpu.VMEM((4, 4, 2, 1, count), F32),
                pltpu.VMEM((3, 1, count), F32),
                pltpu.VMEM((3, 8, 1, count), F32),
                pltpu.VMEM((3, 4, 1, count), F32),
                dma((2,)),
                dma((2, 5, 4)),
                dma((2, 5, 4)),
                dma((2, 6, 4)),
                dma((2, 6, 4)),
                dma((4,)),
                dma((4,)),
                dma((2, 3)),
                dma((2, 3)),
                dma((3, 8)),
                dma((3, 8)),
                dma((2, 3)),
                dma((2, 3)),
            ],
            compiler_params=pltpu.CompilerParams(
                collective_id=0, has_side_effects=True, vmem_limit_bytes=60 * 1024 * 1024
            ),
        )(pairings, logit_scale, embeddings[0])
        return grad[None], loss

    return jax.shard_map(
        shards,
        mesh=mesh,
        in_specs=(P("mod", "dp", None), P(), P()),
        out_specs=(P("mod", "dp", None), P("mod", "dp")),
        check_vma=False,
    )
```
